32 devices in a mesh: groups: 2 (over y), dp: 4 (over z), tgt: 4 (over x, core).
Axes of the slice: x: 2, y: 2, z: 4, core: 2. Of those that a mesh axis runs over, the one named last changes fastest.
Arguments:
- hidden: bfloat16 [6144, 4096], P(('groups', 'dp', 'tgt')), parts along dimension 0, may hold values from -6 to 6
- cotangent: bfloat16 [6144, 4096], P(('groups', 'dp', 'tgt')), parts along dimension 0, may hold values from -6 to 6
- adapter_down_weight: bfloat16 [4096, 64], replicated, may hold values from -0.09375 to 0.09375
- adapter_up_weight: bfloat16 [64, 4096], replicated, may hold values from -0.75 to 0.75
- width_projection_factor: bfloat16 [4096, 512], replicated, may hold values from -0.09375 to 0.09375
- rank_projection_factor: bfloat16 [64, 8], replicated, may hold values from -0.75 to 0.75
- targets: bfloat16 [8, 768, 8192], P(('groups', 'dp'), 'tgt'), parts along dimension 0, may hold values from -100 to 100
- strata: int32 [768], P(('groups', 'dp', 'tgt')), parts along dimension 0, may hold values from 0 to 31
- keep: int32 [768], P(('groups', 'dp', 'tgt')), parts along dimension 0, may hold values from 0 to 1
- shard_example_count: int32 [32], P(('groups', 'dp', 'tgt')), parts along dimension 0, may hold values from 18 to 24
- stratum_owner_table: int32 [32], replicated, may hold values from 0 to 3, as said below
Outputs:
- selection: float32 [768], P(('groups', 'dp', 'tgt')), parts along dimension 0
The draws below stay inside these ranges and needn't reach their ends.
There are 2 independent parts, one for each index of `groups`. The reference program is written for one: setup_inputs(seed, part) draws one part's arguments, and reference() takes and returns one part's arrays. A program takes and returns all parts, laid end to end along the dimension named above; an argument that names none is the same for every part. Nothing has to cross between parts.
Inputs may be any that keep to these rules, and one draw needn't show every extreme that they name: `stratum_owner_table`: each of the 4 owners holds exactly 8 strata.
All inputs are finite; a program needn't handle non-finite values.
Results may differ from the reference program's by a relative error of at most 0.0029.
Values may be sent and summed in bfloat16 or wider, within the bound.
A program may use at most 64 MiB of HBM per device.

```python
import math
import jax
import jax.numpy as jnp
import numpy as np
from jax import lax

MODEL_WIDTH = 4096
ADAPTER_RANK = 64
KD = 512
KR = 8
FEAT = 8192
SEQ = 8
EX_DEV = 24
CAP = 2
TGT = 768
TASKS = 16
OWNERS = 4
NSTRATA = 32
SHARDS = 16
EXAMPLES = 384
TOKENS = 3072


def draw_keep(key, part):
    position = jnp.arange(EXAMPLES, dtype=jnp.int32)
    threshold = 330 + 670 * position // EXAMPLES
    ticket = jax.random.randint(key, (EXAMPLES,), 0, 1000, dtype=jnp.int32)
    return (ticket < threshold).astype(jnp.int32)


def draw_shard_example_count(key, part):
    drawn_counts = jax.random.randint(key, (SHARDS,), max(1, 3 * EX_DEV // 4), EX_DEV + 1, dtype=jnp.int32)
    chosen = jax.random.randint(jax.random.fold_in(key, 7), (), 0, SHARDS, dtype=jnp.int32)
    return jnp.where(jnp.arange(SHARDS, dtype=jnp.int32) == chosen, EX_DEV, drawn_counts).astype(jnp.int32)


def draw_stratum_owner_table(key, part):
    shuffled = jax.random.permutation(key, NSTRATA).astype(jnp.int32)
    return (shuffled % OWNERS).astype(jnp.int32)


def draw_targets(key, part):
    per_task = TGT // TASKS
    centers = jax.random.normal(jax.random.fold_in(key, 1), (OWNERS, TASKS, 1, FEAT), jnp.float32)
    target_noise = jax.random.normal(jax.random.fold_in(key, 2), (OWNERS, TASKS, per_task, FEAT), jnp.float32)
    values = centers + target_noise
    return values.reshape(OWNERS, TGT, FEAT).astype(jnp.bfloat16)


def with_ends(values, own_key, least, largest):
    spot = [jax.random.randint(jax.random.fold_in(own_key, axis), (), 0, length) for axis, length in enumerate(values.shape)]
    widest = values.shape.index(max(values.shape))
    neighbour = spot[:widest] + [(spot[widest] + 1) % values.shape[widest]] + spot[widest + 1:]
    return values.at[tuple(spot)].set(least).at[tuple(neighbour)].set(largest)


def steps_of(rng, dims, cuts, low, top_value):
    def one(axis_at, parts):
        heights = jax.random.uniform(jax.random.fold_in(jax.random.fold_in(rng, 6), axis_at), (parts,), jnp.float32, low / len(cuts), top_value / len(cuts))
        return jnp.repeat(jnp.exp(heights), dims[axis_at] // parts).reshape((-1,) + (1,) * (len(dims) - axis_at - 1))

    loudness = one(*cuts[0])
    for cut in cuts[1:]:
        loudness = loudness * one(*cut)
    return loudness


def rank_bounds(amount, slope):
    loads = [(1 << 20) // math.isqrt(standing ** slope) + 1 for standing in range(1, amount + 1)]
    scale = 1 + sum(loads) // (1 << 30)
    return np.cumsum(np.array([max(1, weight // scale) for weight in loads]))


def ranked(own_key, dims, number_of, lean):
    grid = rank_bounds(number_of, lean)
    lot = jax.random.randint(jax.random.fold_in(own_key, 1), dims, 0, int(grid[number_of - 1]))
    rank = jnp.searchsorted(jnp.asarray(grid, jnp.int32), lot, side="right")
    return jax.random.permutation(jax.random.fold_in(own_key, 2), number_of)[rank].astype(jnp.int32)


def bell_draw(stream_key, dims, scale, reach, pieces=(), kind=jnp.bfloat16):
    values = jax.random.normal(stream_key, dims, jnp.float32) * scale
    if len(pieces) > 0:
        values = steps_of(stream_key, dims, pieces, -0.22, 0.18) * values
    return jnp.clip(values, min=-reach, max=reach).astype(kind)


def setup_inputs(seed: int = 0, part: int = 0) -> dict:
    splits = jax.random.split(jax.random.key(seed), 12)
    own_keys = jax.random.split(jax.random.fold_in(splits[11], part), 12)
    hidden = bell_draw(own_keys[0], (TOKENS, MODEL_WIDTH), 1.0, 6.0, ((0, 16),))
    cotangent = bell_draw(own_keys[1], (TOKENS, MODEL_WIDTH), 1.0, 6.0, ((0, 16),))
    adapter_down_weight = bell_draw(splits[2], (MODEL_WIDTH, ADAPTER_RANK), MODEL_WIDTH ** -0.5, 0.09375)
    adapter_up_weight = bell_draw(splits[3], (ADAPTER_RANK, MODEL_WIDTH), ADAPTER_RANK ** -0.5, 0.75)
    width_projection_factor = bell_draw(splits[4], (MODEL_WIDTH, KD), MODEL_WIDTH ** -0.5, 0.09375)
    rank_projection_factor = bell_draw(splits[5], (ADAPTER_RANK, KR), ADAPTER_RANK ** -0.5, 0.75)
    targets = draw_targets(jax.random.fold_in(jax.random.fold_in(splits[11], part), 71), part)
    strata = with_ends(ranked(own_keys[7], (EXAMPLES,), NSTRATA, 2), jax.random.fold_in(own_keys[7], 3), 0, NSTRATA - 1).astype(jnp.int32)
    keep = draw_keep(jax.random.fold_in(jax.random.fold_in(splits[11], part), 71), part)
    shard_example_count = draw_shard_example_count(jax.random.fold_in(jax.random.fold_in(splits[11], part), 71), part)
    stratum_owner_table = draw_stratum_owner_table(jax.random.fold_in(splits[11], 71), part)
    return dict(hidden=hidden, cotangent=cotangent, adapter_down_weight=adapter_down_weight, adapter_up_weight=adapter_up_weight, width_projection_factor=width_projection_factor, rank_projection_factor=rank_projection_factor, targets=targets, strata=strata, keep=keep, shard_example_count=shard_example_count, stratum_owner_table=stratum_owner_table)


def per_example(values):
    return values.astype(jnp.float32).reshape(EXAMPLES, SEQ, values.shape[1])

def reference(hidden, cotangent, adapter_down_weight, adapter_up_weight, width_projection_factor, rank_projection_factor, targets, strata, keep, shard_example_count, stratum_owner_table):
    shards = EXAMPLES // EX_DEV
    position = jnp.arange(EXAMPLES, dtype=jnp.int32)
    home_shard = position // EX_DEV
    local_pos = position % EX_DEV
    usable = local_pos < shard_example_count[home_shard]
    is_live = jnp.logical_and(keep == 1, usable)
    counts = jnp.zeros((NSTRATA,), jnp.float32).at[strata].add(is_live.astype(jnp.float32))
    down_activation = jnp.dot(hidden, adapter_down_weight, preferred_element_type=jnp.float32).astype(jnp.bfloat16)
    up_backward_product = jnp.dot(cotangent, adapter_up_weight.T, preferred_element_type=jnp.float32).astype(jnp.bfloat16)
    wide_hidden = jnp.dot(hidden, width_projection_factor, preferred_element_type=jnp.float32).astype(jnp.bfloat16)
    wide_back = jnp.dot(cotangent, width_projection_factor, preferred_element_type=jnp.float32).astype(jnp.bfloat16)
    rank_down = jnp.dot(down_activation, rank_projection_factor, preferred_element_type=jnp.float32).astype(jnp.bfloat16)
    rank_up = jnp.dot(up_backward_product, rank_projection_factor, preferred_element_type=jnp.float32).astype(jnp.bfloat16)
    up_grad = jnp.einsum('esr,esd->erd', per_example(rank_down), per_example(wide_back), precision=lax.Precision.HIGHEST)
    down_grad = jnp.einsum('esd,esr->edr', per_example(wide_hidden), per_example(rank_up), precision=lax.Precision.HIGHEST)
    features = jnp.concatenate([up_grad.reshape(EXAMPLES, KR * KD), down_grad.reshape(EXAMPLES, KD * KR)], axis=1).astype(jnp.bfloat16)
    owner_of = stratum_owner_table[strata]
    owner_blocks = owner_of.reshape(shards, EX_DEV)
    live_blocks = is_live.reshape(shards, EX_DEV)
    ordinal = jnp.arange(EX_DEV, dtype=jnp.int32)
    earlier = ordinal[None, :, None] > ordinal[None, None, :]
    same_owner = owner_blocks[:, :, None] == owner_blocks[:, None, :]
    ahead = jnp.logical_and(jnp.logical_and(earlier, same_owner), live_blocks[:, None, :])
    slot_rank = lax.optimization_barrier(jnp.sum(ahead.astype(jnp.int32), axis=2)).reshape(EXAMPLES)
    is_sent = jnp.logical_and(is_live, slot_rank < CAP)
    bounded_rank = jnp.minimum(slot_rank, CAP - 1)
    slot_owner = jnp.where(is_sent, owner_of, OWNERS)
    slot_table = jnp.zeros((OWNERS, shards, CAP), jnp.int32).at[slot_owner, home_shard, bounded_rank].set(position, mode='drop')
    per_task = TGT // TASKS
    task_mask = ((jnp.arange(TGT, dtype=jnp.int32) // per_task)[:, None] == jnp.arange(TASKS, dtype=jnp.int32)[None, :]).astype(jnp.float32)

    def score_owner(owner_args):
        rows_index, owner_targets = owner_args
        chosen_rows = features[rows_index.reshape(-1)].astype(jnp.float32)
        target_values = owner_targets.astype(jnp.float32)
        row_inv = lax.rsqrt(lax.optimization_barrier(jnp.sum(chosen_rows * chosen_rows, axis=1)) + 1e-06)
        target_inv = lax.rsqrt(lax.optimization_barrier(jnp.sum(target_values * target_values, axis=1)) + 1e-06)
        products = lax.dot_general(chosen_rows, target_values, (((1,), (1,)), ((), ())), precision=lax.Precision.HIGHEST)
        aligned = math.sqrt(FEAT) * products * row_inv[:, None] * target_inv[None, :]
        task_sums = jnp.dot(jnp.maximum(aligned, 0.0), task_mask, precision=lax.Precision.HIGHEST)
        return lax.optimization_barrier(jnp.max(task_sums / per_task, axis=1))
    raw_table = lax.map(score_owner, (slot_table, targets))
    raw_score = raw_table.reshape(OWNERS, shards, CAP)[owner_of, home_shard, bounded_rank]
    stratum_count = counts[strata]
    weight = jnp.sqrt(jnp.sum(counts) / (NSTRATA * jnp.maximum(stratum_count, 1.0)))
    return jnp.where(is_sent, raw_score * weight, 0.0)
```

```python
import math

import jax
import jax.numpy as jnp
from jax import lax
from jax.experimental import pallas as pl
from jax.experimental.pallas import tpu as pltpu
from jax.sharding import PartitionSpec as P

CAP = 2
TASKS = 16
EPSILON = 1e-06
CORES = 2
CHUNKS = 4
HALVES = 2

F32 = jnp.float32
BF16 = jnp.bfloat16
I32 = jnp.int32
MESH = pl.DeviceIdType.MESH


def dot(a, b):
    return jnp.dot(a, b, preferred_element_type=F32)


def dot_nt(a, b):
    return lax.dot_general(a, b, (((1,), (1,)), ((), ())), preferred_element_type=F32)


def iota(shape, axis):
    return lax.broadcasted_iota(I32, shape, axis)


def column_of(row):
    size = row.shape[1]
    eye = iota((size, size), 0) == iota((size, size), 1)
    return jnp.sum(jnp.where(eye, jnp.broadcast_to(row, (size, size)), 0.0), axis=1, keepdims=True)


def each(start, stop, body):
    if stop - start <= 32:
        for k in range(start, stop):
            body(k)
    else:
        lax.fori_loop(start, stop, lambda k, c: (body(k), c)[1], 0)


def partner(z, k, nz):
    if nz & (nz - 1):
        return lax.rem(z + k, nz)
    bit = 1
    while bit < nz:
        if k & bit:
            z = z + bit - 2 * bit * lax.rem(z // bit, 2)
        bit *= 2
    return z


def kernel(nz, nt, hid_h, cot_h, ad_h, au_h, w_h, rp_ref, tg_h, strata_ref, keep_ref,
           cnt_ref, table_ref, out_ref, hid, cot, ad, au, wf, tup, tdr, tdn, sel, sbuf, xbuf,
           acc, crow, cbuf, rrow, rbuf, in_sem, tg_sem, zs, zr, xs, xr, cs, cr, ns, nr, rs, rr):
    n = nz * nt
    nx = nt // CORES
    z = lax.axis_index("dp")
    t = lax.axis_index("tgt")
    me = z * nt + t
    x, c = t // CORES, lax.rem(t, CORES)
    tokens, width = hid.shape
    kd = wf.shape[1]
    hw = kd // HALVES
    kr = rp_ref.shape[1]
    examples = strata_ref.shape[1]
    seq = tokens // examples
    strata_total = table_ref.shape[1]
    local_targets = tdr.shape[0]
    slots = nz * CAP
    rows = slots * kr
    kc = width // CHUNKS

    def peer(j):
        return {"dp": j // nt, "tgt": lax.rem(j, nt)}

    def loads(k):
        ks = pl.ds(k * kc, kc)
        return [
            pltpu.make_async_copy(hid_h.at[:, ks], hid.at[:, ks], in_sem.at[0, k]),
            pltpu.make_async_copy(w_h.at[ks, pl.ds(0, hw)], wf.at[ks, pl.ds(0, hw)], in_sem.at[1, k]),
            pltpu.make_async_copy(cot_h.at[:, ks], cot.at[:, ks], in_sem.at[2, k]),
            pltpu.make_async_copy(ad_h.at[ks, :], ad.at[ks, :], in_sem.at[3, k]),
            pltpu.make_async_copy(au_h.at[:, ks], au.at[:, ks], in_sem.at[4, k]),
        ]

    def late_loads(k):
        ks = pl.ds(k * kc, kc)
        rest = pl.ds(hw, kd - hw)
        return [pltpu.make_async_copy(w_h.at[ks, rest], wf.at[ks, rest], in_sem.at[5, k])]

    first = [loads(k) for k in range(CHUNKS)]
    second = [late_loads(k) for k in range(CHUNKS)]
    up_len = kr * kd
    target_loads = [
        pltpu.make_async_copy(tg_h.at[0, :, pl.ds(r * kd, kd)], tup.at[r], tg_sem.at[r])
        for r in range(kr)
    ] + [pltpu.make_async_copy(tg_h.at[0, :, pl.ds(up_len, up_len)], tdr, tg_sem.at[kr])]
    for group in first + second:
        for copy in group:
            copy.start()
    for copy in target_loads:
        copy.start()

    barrier = pltpu.get_barrier_semaphore()

    def greet(k):
        pl.semaphore_signal(barrier, inc=1, device_id=peer(lax.rem(me + k, n)), device_id_type=MESH)

    each(1, n, greet)

    strata = strata_ref[...].astype(F32)
    live = jnp.logical_and(keep_ref[...] == 1, iota((1, examples), 1) < cnt_ref[...])
    live_f = live.astype(F32)
    strata_c = column_of(strata)
    live_c = column_of(live_f)
    table_c = column_of(table_ref[...].astype(F32))
    member = strata == iota((strata_total, examples), 0).astype(F32)
    owner = jnp.sum(jnp.where(member, table_c, 0.0), axis=0, keepdims=True)
    owner_c = column_of(owner)
    earlier = iota((examples, examples), 0) < iota((examples, examples), 1)
    ahead = jnp.where(jnp.logical_and(earlier, owner_c == owner), live_c, 0.0)
    slot_rank = jnp.sum(ahead, axis=0, keepdims=True)
    sent = jnp.logical_and(live, slot_rank < float(CAP))
    slot = jnp.where(sent, owner * float(CAP) + slot_rank, -1.0)
    lanes = crow.shape[1]
    member_t = strata_c == iota((examples, lanes), 1).astype(F32)
    crow[...] = jnp.sum(jnp.where(member_t, live_c, 0.0), axis=0, keepdims=True)
    own_counts = crow[...]

    spread = (iota((examples, tokens), 1) // seq == iota((examples, tokens), 0)).astype(BF16)
    slot_tok = dot(jnp.broadcast_to(slot, (8, examples)).astype(BF16), spread)[0:1, :]
    row_slot = (iota((rows, tokens), 0) // kr).astype(F32)
    picked = row_slot == slot_tok
    row_rank = (
        lax.rem(iota((rows, kr), 0), kr) == iota((rows, kr), 1)
    ).astype(BF16)

    pl.semaphore_wait(barrier, n - 1)

    def count_copy(k):
        return pltpu.make_async_remote_copy(
            crow, cbuf.at[me], ns, nr, device_id=peer(lax.rem(me + k, n)), device_id_type=MESH)

    each(1, n, lambda k: count_copy(k).start())
    cbuf[me] = own_counts

    span = sel.shape[0]
    dd = span // kr
    src = iota((span, span), 0)
    dst = iota((span, span), 1)
    sel[...] = (src == lax.rem(dst, dd) * kr + dst // dd).astype(F32).astype(BF16)

    wide_h = wide_b = down = up = None
    for k in range(CHUNKS):
        for copy in first[k]:
            copy.wait()
        ks = pl.ds(k * kc, kc)
        h, b, w = hid[:, ks], cot[:, ks], wf[ks, 0:hw]
        terms = (dot(h, w), dot(b, w), dot(h, ad[ks, :]), dot_nt(b, au[:, ks]))
        if k == 0:
            wide_h, wide_b, down, up = terms
        else:
            wide_h, wide_b, down, up = [
                a + p for a, p in zip((wide_h, wide_b, down, up), terms)]
    rank_down = dot(down.astype(BF16), rp_ref[...]).astype(BF16)
    rank_up = dot(up.astype(BF16), rp_ref[...]).astype(BF16)
    mix_up = jnp.where(picked, dot_nt(row_rank, rank_down), 0.0).astype(BF16)
    mix_down = jnp.where(picked, dot_nt(row_rank, rank_up), 0.0).astype(BF16)

    def z_copy(half, k):
        to = partner(z, k, nz)
        return pltpu.make_async_remote_copy(
            sbuf.at[half, to], xbuf.at[half, c, x, z], zs.at[half], zr.at[half, z],
            device_id={"dp": to}, device_id_type=MESH)

    def x_copy(half, src_ref, origin_z, to_x):
        return pltpu.make_async_remote_copy(
            src_ref, xbuf.at[half, c, x, origin_z], xs.at[half], xr.at[half, x, origin_z],
            device_id={"tgt": to_x * CORES + c}, device_id_type=MESH)

    def c_copy(half, src_ref, origin_x, origin_z):
        return pltpu.make_async_remote_copy(
            src_ref, xbuf.at[half, c, origin_x, origin_z], cs.at[half], cr.at[half],
            device_id={"tgt": x * CORES + 1 - c}, device_id_type=MESH)

    def spread_out(half, src_ref, origin_z):
        for dx in range(1, nx):
            x_copy(half, src_ref, origin_z, lax.rem(x + dx, nx)).start()
        c_copy(half, src_ref, x, origin_z).start()

    def features(half, wb, wh):
        up_f = dot(mix_up, wb.astype(BF16)).astype(BF16)
        down_f = dot(mix_down, wh.astype(BF16)).astype(BF16)
        sbuf[half, :, :, 0:hw] = up_f.reshape(nz, CAP * kr, hw)
        sbuf[half, :, :, hw:2 * hw] = down_f.reshape(nz, CAP * kr, hw)
        for k in range(nz - 1, 0, -1):
            z_copy(half, k).start()
        spread_out(half, sbuf.at[half, z], z)
        xbuf[half, c, x, z] = sbuf[half, z]
        wide_u, wide_d = up_f.astype(F32), down_f.astype(F32)
        return jnp.sum(wide_u * wide_u + wide_d * wide_d, axis=1, keepdims=True)

    square = features(0, wide_b, wide_h)
    for k in range(CHUNKS):
        for copy in second[k]:
            copy.wait()
        ks = pl.ds(k * kc, kc)
        w = wf[ks, hw:kd]
        terms = (dot(hid[:, ks], w), dot(cot[:, ks], w))
        if k == 0:
            wide_h, wide_b = terms
        else:
            wide_h, wide_b = wide_h + terms[0], wide_b + terms[1]
    square = square + features(1, wide_b, wide_h)

    for copy in target_loads:
        copy.wait()
    total = None
    for r in range(kr):
        v = tup[r].astype(F32)
        total = v * v if total is None else total + v * v
    for q in range(up_len // kd):
        v = tdr[:, q * kd:(q + 1) * kd].astype(F32)
        total = total + v * v
    target_scale = math.sqrt(2.0 * up_len) * lax.rsqrt(
        jnp.sum(total, axis=1, keepdims=True) + EPSILON)

    def arrange(q):
        piece = dot(tdr[:, q * span:(q + 1) * span], sel[...]).astype(BF16)
        for r in range(kr):
            tdn[r, :, q * dd:(q + 1) * dd] = piece[:, r * dd:(r + 1) * dd]

    def relay_z(half, k):
        origin = partner(z, k, nz)
        pltpu.make_async_remote_copy(
            sbuf.at[half, origin], xbuf.at[half, c, x, origin], zs.at[half], zr.at[half, origin],
            device_id={"dp": origin}, device_id_type=MESH).wait_recv()
        spread_out(half, xbuf.at[half, c, x, origin], origin)

    def relay_x(half, dx, k):
        origin_x = lax.rem(x + dx, nx)
        origin_z = partner(z, k, nz)
        block = xbuf.at[half, c, origin_x, origin_z]
        pltpu.make_async_remote_copy(
            block, block, xs.at[half], xr.at[half, origin_x, origin_z],
            device_id={"tgt": origin_x * CORES + c}, device_id_type=MESH).wait_recv()
        c_copy(half, block, origin_x, origin_z).start()

    pieces = up_len // span
    todo = [lambda q=q: arrange(q) for q in range(pieces)]
    steps = []
    for half in range(HALVES):
        steps += [lambda half=half, k=k: relay_z(half, k) for k in range(1, nz)]
    done = 0
    for i, step in enumerate(steps):
        while done < pieces and done * len(steps) <= i * pieces:
            todo[done]()
            done += 1
        step()
    while done < pieces:
        todo[done]()
        done += 1
    for half in range(HALVES):
        for dx in range(1, nx):
            for k in range(nz):
                relay_x(half, dx, k)

    count = nx * nz * CORES * CAP * kr
    lane = iota((local_targets, count), 1)
    lane_rank = lax.rem(lane, kr)
    for half in range(HALVES):
        other = xbuf.at[half, 1 - c]
        pltpu.make_async_copy(other, other, cr.at[half]).wait()
        block = xbuf[half].reshape(count, 2 * hw)
        cols = slice(half * hw, (half + 1) * hw)
        left = tup[:, :, cols].reshape(kr * local_targets, hw)
        right = tdn[:, :, cols].reshape(kr * local_targets, hw)
        products = dot_nt(left, block[:, 0:hw]) + dot_nt(right, block[:, hw:2 * hw])
        products = products.reshape(kr, local_targets, count)
        s = products[0]
        for r in range(1, kr):
            s = jnp.where(lane_rank == r, products[r], s)
        if half == 0:
            acc[...] = s
        else:
            s = acc[...] + s
    shift = 1
    while shift < kr:
        s = s + pltpu.roll(s, count - shift, 1)
        shift *= 2
    per_task = local_targets * nt // TASKS
    s = jnp.maximum(s * target_scale, 0.0)
    local_tasks = local_targets // per_task
    best = jnp.sum(s[0:per_task], axis=0, keepdims=True)
    for k in range(1, local_tasks):
        best = jnp.maximum(
            best, jnp.sum(s[k * per_task:(k + 1) * per_task], axis=0, keepdims=True))
    rrow[...] = best / float(per_task)

    def score_copy(k):
        return pltpu.make_async_remote_copy(
            rrow, rbuf.at[me], rs, rr, device_id=peer(lax.rem(me + k, n)), device_id_type=MESH)

    each(1, n, lambda k: score_copy(k).start())
    rbuf[me] = rrow[...]

    counts_all = cbuf.at[pl.ds(0, n - 1)]
    pltpu.make_async_copy(counts_all, counts_all, nr).wait()
    counts = jnp.sum(cbuf[...], axis=0)
    overall = jnp.sum(counts, axis=1, keepdims=True)
    stratum_c = jnp.sum(jnp.where(member_t, counts, 0.0), axis=1, keepdims=True)
    weight_c = jnp.sqrt(overall / (float(strata_total) * jnp.maximum(stratum_c, 1.0)))
    eye = iota((examples, examples), 0) == iota((examples, examples), 1)
    weight = jnp.sum(jnp.where(eye, weight_c, 0.0), axis=0, keepdims=True)
    at_slot = (iota((rows, examples), 0) // kr).astype(F32) == slot
    square_e = jnp.sum(jnp.where(at_slot, square, 0.0), axis=0, keepdims=True)
    weight = weight * lax.rsqrt(square_e + EPSILON)

    scores_all = rbuf.at[pl.ds(0, n - 1)]
    pltpu.make_async_copy(scores_all, scores_all, rr).wait()
    home = ((c * nx + x) * nz + z) * CAP * kr
    raw = jnp.zeros((1, examples), F32)
    lane_row = iota((1, count), 1)
    for o in range(nz):
        top = jnp.max(rbuf[o * nt:(o + 1) * nt], axis=0)
        for rank in range(CAP):
            mine = jnp.sum(
                jnp.where(lane_row == home + rank * kr, top, 0.0), axis=1, keepdims=True)
            raw = jnp.where(slot == float(o * CAP + rank), mine, raw)
    out_ref[...] = jnp.where(sent, raw * weight, 0.0)

    def drain(ref, sem):
        pltpu.make_async_copy(ref, ref, sem).wait()

    drain(counts_all, ns)
    drain(scores_all, rs)
    for half in range(HALVES):
        if nz > 1:
            drain(sbuf.at[half, pl.ds(0, nz - 1)], zs.at[half])
        for _ in range(1, nx):
            drain(xbuf.at[half, 0, 0], xs.at[half])
        drain(xbuf.at[half, 0], cs.at[half])


def solution(mesh):
    nz, nt = mesh.shape["dp"], mesh.shape["tgt"]

    def shards(hidden, cotangent, adapter_down_weight, adapter_up_weight, width_projection_factor,
               rank_projection_factor, targets, strata, keep, shard_example_count,
               stratum_owner_table):
        tokens, width = hidden.shape
        rank, kr = rank_projection_factor.shape
        kd = width_projection_factor.shape[1]
        examples = strata.shape[0]
        strata_total = stratum_owner_table.shape[0]
        local_targets, feat = targets.shape[1:]
        n, nx = nz * nt, nt // CORES
        count = n * CAP * kr
        span = kr * 128
        count_lanes = -(-strata_total // 128) * 128
        dma = pltpu.SemaphoreType.DMA
        hbm = pl.BlockSpec(memory_space=pl.ANY)
        vmem = pl.BlockSpec(memory_space=pltpu.VMEM)

        def body(*refs):
            kernel(nz, nt, *refs)

        out = pl.pallas_call(
            body,
            name="select",
            out_shape=jax.ShapeDtypeStruct((1, examples), F32),
            in_specs=[hbm, hbm, hbm, hbm, hbm, vmem, hbm, vmem, vmem, vmem, vmem],
            out_specs=vmem,
            scratch_shapes=[
                pltpu.VMEM((tokens, width), BF16),
                pltpu.VMEM((tokens, width), BF16),
                pltpu.VMEM((width, rank), BF16),
                pltpu.VMEM((rank, width), BF16),
                pltpu.VMEM((width, kd), BF16),
                pltpu.VMEM((kr, local_targets, kd), BF16),
                pltpu.VMEM((local_targets, feat // 2), BF16),
                pltpu.VMEM((kr, local_targets, kd), BF16),
                pltpu.VMEM((span, span), BF16),
                pltpu.VMEM((HALVES, nz, CAP * kr, 2 * kd // HALVES), BF16),
                pltpu.VMEM((HALVES, CORES, nx, nz, CAP * kr, 2 * kd // HALVES), BF16),
                pltpu.VMEM((local_targets, count), F32),
                pltpu.VMEM((1, count_lanes), F32),
                pltpu.VMEM((n, 1, count_lanes), F32),
                pltpu.VMEM((1, count), F32),
                pltpu.VMEM((n, 1, count), F32),
                dma((6, CHUNKS)),
                dma((kr + 1,)),
                dma((HALVES,)),
                dma((HALVES, nz)),
                dma((HALVES,)),
                dma((HALVES, nx, nz)),
                dma((HALVES,)),
                dma((HALVES,)),
                dma,
                dma,
                dma,
                dma,
            ],
            compiler_params=pltpu.CompilerParams(
                collective_id=0, has_side_effects=True, vmem_limit_bytes=60 * 1024 * 1024),
        )(hidden, cotangent, adapter_down_weight, adapter_up_weight, width_projection_factor,
          rank_projection_factor, targets, strata.reshape(1, -1), keep.reshape(1, -1),
          shard_example_count.reshape(1, 1), stratum_owner_table.reshape(1, -1))
        return out.reshape(-1)

    split = P(("groups", "dp", "tgt"))
    rows = P(("groups", "dp", "tgt"), None)
    return jax.shard_map(
        shards,
        mesh=mesh,
        in_specs=(rows, rows, P(), P(), P(), P(), P(("groups", "dp"), "tgt", None),
                  split, split, split, P()),
        out_specs=split,
        check_vma=False,
    )
```

```python
import math

import jax
import jax.numpy as jnp
from jax import lax
from jax.experimental import pallas as pl
from jax.experimental.pallas import tpu as pltpu
from jax.sharding import PartitionSpec as P

CAP = 2
TASKS = 16
EPSILON = 1e-06
CORES = 2
CHUNKS = 4
HALVES = 2

F32 = jnp.float32
BF16 = jnp.bfloat16
I32 = jnp.int32
MESH = pl.DeviceIdType.MESH


def dot(a, b):
    return jnp.dot(a, b, preferred_element_type=F32)


def dot_nt(a, b):
    return lax.dot_general(a, b, (((1,), (1,)), ((), ())), preferred_element_type=F32)


def iota(shape, axis):
    return lax.broadcasted_iota(I32, shape, axis)


def column_of(row):
    size = row.shape[1]
    eye = iota((size, size), 0) == iota((size, size), 1)
    return jnp.sum(jnp.where(eye, jnp.broadcast_to(row, (size, size)), 0.0), axis=1, keepdims=True)


def each(start, stop, body):
    if stop - start <= 32:
        for k in range(start, stop):
            body(k)
    else:
        lax.fori_loop(start, stop, lambda k, c: (body(k), c)[1], 0)


def partner(z, k, nz):
    if nz & (nz - 1):
        return lax.rem(z + k, nz)
    bit = 1
    while bit < nz:
        if k & bit:
            z = z + bit - 2 * bit * lax.rem(z // bit, 2)
        bit *= 2
    return z


def kernel(nz, nt, hid_h, cot_h, ad_h, au_h, w_h, rp_ref, tg_h, strata_ref, keep_ref,
           cnt_ref, table_ref, out_ref, hid, cot, ad, au, wf, tup, tdr, tdn, sel, sbuf, xbuf,
           acc, crow, cbuf, rrow, rbuf, in_sem, tg_sem, zs, zr, xs, xr, cs, cr, ns, nr, rs, rr):
    n = nz * nt
    nx = nt // CORES
    z = lax.axis_index("dp")
    t = lax.axis_index("tgt")
    me = z * nt + t
    x, c = t // CORES, lax.rem(t, CORES)
    tokens, width = hid.shape
    kd = wf.shape[1]
    hw = kd // HALVES
    kr = rp_ref.shape[0]
    examples = strata_ref.shape[1]
    seq = tokens // examples
    strata_total = table_ref.shape[1]
    local_targets = tdr.shape[0]
    slots = nz * CAP
    rows = slots * kr
    kc = width // CHUNKS

    def peer(j):
        return {"dp": j // nt, "tgt": lax.rem(j, nt)}

    def loads(k):
        ks = pl.ds(k * kc, kc)
        return [
            pltpu.make_async_copy(hid_h.at[:, ks], hid.at[:, ks], in_sem.at[0, k]),
            pltpu.make_async_copy(w_h.at[ks, pl.ds(0, hw)], wf.at[ks, pl.ds(0, hw)], in_sem.at[1, k]),
            pltpu.make_async_copy(cot_h.at[:, ks], cot.at[:, ks], in_sem.at[2, k]),
            pltpu.make_async_copy(ad_h.at[:, ks], ad.at[:, ks], in_sem.at[3, k]),
            pltpu.make_async_copy(au_h.at[:, ks], au.at[:, ks], in_sem.at[4, k]),
        ]

    def late_loads(k):
        ks = pl.ds(k * kc, kc)
        rest = pl.ds(hw, kd - hw)
        return [pltpu.make_async_copy(w_h.at[ks, rest], wf.at[ks, rest], in_sem.at[5, k])]

    first = [loads(k) for k in range(CHUNKS)]
    second = [late_loads(k) for k in range(CHUNKS)]
    up_len = kr * kd
    target_loads = [
        pltpu.make_async_copy(tg_h.at[0, :, pl.ds(r * kd, kd)], tup.at[r], tg_sem.at[r])
        for r in range(kr)
    ] + [pltpu.make_async_copy(tg_h.at[0, :, pl.ds(up_len, up_len)], tdr, tg_sem.at[kr])]
    for group in first + second:
        for copy in group:
            copy.start()
    for copy in target_loads:
        copy.start()

    barrier = pltpu.get_barrier_semaphore()

    def greet(k):
        pl.semaphore_signal(barrier, inc=1, device_id=peer(lax.rem(me + k, n)), device_id_type=MESH)

    each(1, n, greet)

    strata = strata_ref[...].astype(F32)
    live = jnp.logical_and(keep_ref[...] == 1, iota((1, examples), 1) < cnt_ref[0])
    live_f = live.astype(F32)
    strata_c = column_of(strata)
    live_c = column_of(live_f)
    table_c = column_of(table_ref[...].astype(F32))
    member = strata == iota((strata_total, examples), 0).astype(F32)
    owner = jnp.sum(jnp.where(member, table_c, 0.0), axis=0, keepdims=True)
    owner_c = column_of(owner)
    earlier = iota((examples, examples), 0) < iota((examples, examples), 1)
    ahead = jnp.where(jnp.logical_and(earlier, owner_c == owner), live_c, 0.0)
    slot_rank = jnp.sum(ahead, axis=0, keepdims=True)
    sent = jnp.logical_and(live, slot_rank < float(CAP))
    slot = jnp.where(sent, owner * float(CAP) + slot_rank, -1.0)
    lanes = crow.shape[1]
    member_t = strata_c == iota((examples, lanes), 1).astype(F32)
    crow[...] = jnp.sum(jnp.where(member_t, live_c, 0.0), axis=0, keepdims=True)
    own_counts = crow[...]

    spread = (iota((examples, tokens), 1) // seq == iota((examples, tokens), 0)).astype(BF16)
    slot_tok = dot(jnp.broadcast_to(slot, (8, examples)).astype(BF16), spread)[0:1, :]
    row_slot = (iota((rows, tokens), 0) // kr).astype(F32)
    picked = row_slot == slot_tok
    row_rank = (
        lax.rem(iota((rows, kr), 0), kr) == iota((rows, kr), 1)
    ).astype(BF16)

    pl.semaphore_wait(barrier, n - 1)

    def count_copy(k):
        return pltpu.make_async_remote_copy(
            crow, cbuf.at[me], ns, nr, device_id=peer(lax.rem(me + k, n)), device_id_type=MESH)

    each(1, n, lambda k: count_copy(k).start())
    cbuf[me] = own_counts

    span = sel.shape[0]
    dd = span // kr
    dst = iota((1, span), 1)
    source = lax.rem(dst, dd) * kr + dst // dd
    sel[...] = (iota((span, span), 0) == source).astype(F32).astype(BF16)

    wide_h = wide_b = down = up = None
    for k in range(CHUNKS):
        for copy in first[k]:
            copy.wait()
        ks = pl.ds(k * kc, kc)
        h, b, w = hid[:, ks], cot[:, ks], wf[ks, 0:hw]
        terms = (dot(h, w), dot(b, w), dot_nt(h, ad[:, ks]), dot_nt(b, au[:, ks]))
        if k == 0:
            wide_h, wide_b, down, up = terms
        else:
            wide_h, wide_b, down, up = [
                a + p for a, p in zip((wide_h, wide_b, down, up), terms)]
    rank_down = dot_nt(down.astype(BF16), rp_ref[...]).astype(BF16)
    rank_up = dot_nt(up.astype(BF16), rp_ref[...]).astype(BF16)
    mix_up = jnp.where(picked, dot_nt(row_rank, rank_down), 0.0).astype(BF16)
    mix_down = jnp.where(picked, dot_nt(row_rank, rank_up), 0.0).astype(BF16)

    def z_copy(half, k):
        to = partner(z, k, nz)
        return pltpu.make_async_remote_copy(
            sbuf.at[half, to], xbuf.at[half, c, x, z], zs.at[half], zr.at[half, z],
            device_id={"dp": to}, device_id_type=MESH)

    def x_copy(half, src_ref, origin_z, to_x):
        return pltpu.make_async_remote_copy(
            src_ref, xbuf.at[half, c, x, origin_z], xs.at[half], xr.at[half, x, origin_z],
            device_id={"tgt": to_x * CORES + c}, device_id_type=MESH)

    def c_copy(half, src_ref, origin_x, origin_z):
        return pltpu.make_async_remote_copy(
            src_ref, xbuf.at[half, c, origin_x, origin_z], cs.at[half], cr.at[half],
            device_id={"tgt": x * CORES + 1 - c}, device_id_type=MESH)

    def spread_out(half, src_ref, origin_z):
        for dx in range(1, nx):
            x_copy(half, src_ref, origin_z, lax.rem(x + dx, nx)).start()
        c_copy(half, src_ref, x, origin_z).start()

    def features(half, wb, wh):
        up_f = dot(mix_up, wb.astype(BF16)).astype(BF16)
        down_f = dot(mix_down, wh.astype(BF16)).astype(BF16)
        sbuf[half, :, :, 0:hw] = up_f.reshape(nz, CAP * kr, hw)
        sbuf[half, :, :, hw:2 * hw] = down_f.reshape(nz, CAP * kr, hw)
        for k in range(nz - 1, 0, -1):
            z_copy(half, k).start()
        spread_out(half, sbuf.at[half, z], z)
        xbuf[half, c, x, z] = sbuf[half, z]
        wide_u, wide_d = up_f.astype(F32), down_f.astype(F32)
        return jnp.sum(wide_u * wide_u + wide_d * wide_d, axis=1, keepdims=True)

    square = features(0, wide_b, wide_h)
    for k in range(CHUNKS):
        for copy in second[k]:
            copy.wait()
        ks = pl.ds(k * kc, kc)
        w = wf[ks, hw:kd]
        terms = (dot(hid[:, ks], w), dot(cot[:, ks], w))
        if k == 0:
            wide_h, wide_b = terms
        else:
            wide_h, wide_b = wide_h + terms[0], wide_b + terms[1]
    square = square + features(1, wide_b, wide_h)

    for copy in target_loads:
        copy.wait()
    total = None
    for r in range(kr):
        v = tup[r].astype(F32)
        total = v * v if total is None else total + v * v
    for q in range(up_len // kd):
        v = tdr[:, q * kd:(q + 1) * kd].astype(F32)
        total = total + v * v
    target_scale = math.sqrt(2.0 * up_len) * lax.rsqrt(
        jnp.sum(total, axis=1, keepdims=True) + EPSILON)

    def arrange(q):
        piece = dot(tdr[:, q * span:(q + 1) * span], sel[...]).astype(BF16)
        for r in range(kr):
            tdn[r, :, q * dd:(q + 1) * dd] = piece[:, r * dd:(r + 1) * dd]

    def relay_z(half, k):
        origin = partner(z, k, nz)
        pltpu.make_async_remote_copy(
            sbuf.at[half, origin], xbuf.at[half, c, x, origin], zs.at[half], zr.at[half, origin],
            device_id={"dp": origin}, device_id_type=MESH).wait_recv()
        spread_out(half, xbuf.at[half, c, x, origin], origin)

    def relay_x(half, dx, k):
        origin_x = lax.rem(x + dx, nx)
        origin_z = partner(z, k, nz)
        block = xbuf.at[half, c, origin_x, origin_z]
        pltpu.make_async_remote_copy(
            block, block, xs.at[half], xr.at[half, origin_x, origin_z],
            device_id={"tgt": origin_x * CORES + c}, device_id_type=MESH).wait_recv()
        c_copy(half, block, origin_x, origin_z).start()

    pieces = up_len // span
    todo = [lambda q=q: arrange(q) for q in range(pieces)]
    steps = []
    for half in range(HALVES):
        steps += [lambda half=half, k=k: relay_z(half, k) for k in range(1, nz)]
    done = 0
    for i, step in enumerate(steps):
        while done < pieces and done * len(steps) <= i * pieces:
            todo[done]()
            done += 1
        step()
    while done < pieces:
        todo[done]()
        done += 1
    for half in range(HALVES):
        for dx in range(1, nx):
            for k in range(nz):
                relay_x(half, dx, k)

    count = nx * nz * CORES * CAP * kr
    lane = iota((local_targets, count), 1)
    lane_rank = lax.rem(lane, kr)
    for half in range(HALVES):
        other = xbuf.at[half, 1 - c]
        pltpu.make_async_copy(other, other, cr.at[half]).wait()
        block = xbuf[half].reshape(count, 2 * hw)
        cols = slice(half * hw, (half + 1) * hw)
        left = tup[:, :, cols].reshape(kr * local_targets, hw)
        right = tdn[:, :, cols].reshape(kr * local_targets, hw)
        products = dot_nt(left, block[:, 0:hw]) + dot_nt(right, block[:, hw:2 * hw])
        products = products.reshape(kr, local_targets, count)
        s = products[0]
        for r in range(1, kr):
            s = jnp.where(lane_rank == r, products[r], s)
        if half == 0:
            acc[...] = s
        else:
            s = acc[...] + s
    shift = 1
    while shift < kr:
        s = s + pltpu.roll(s, count - shift, 1)
        shift *= 2
    per_task = local_targets * nt // TASKS
    s = jnp.maximum(s * target_scale, 0.0)
    local_tasks = local_targets // per_task
    best = jnp.sum(s[0:per_task], axis=0, keepdims=True)
    for k in range(1, local_tasks):
        best = jnp.maximum(
            best, jnp.sum(s[k * per_task:(k + 1) * per_task], axis=0, keepdims=True))
    rrow[...] = best / float(per_task)

    def score_copy(k):
        return pltpu.make_async_remote_copy(
            rrow, rbuf.at[me], rs, rr, device_id=peer(lax.rem(me + k, n)), device_id_type=MESH)

    each(1, n, lambda k: score_copy(k).start())
    rbuf[me] = rrow[...]

    counts_all = cbuf.at[pl.ds(0, n - 1)]
    pltpu.make_async_copy(counts_all, counts_all, nr).wait()
    counts = jnp.sum(cbuf[...], axis=0)
    overall = jnp.sum(counts, axis=1, keepdims=True)
    stratum_c = jnp.sum(jnp.where(member_t, counts, 0.0), axis=1, keepdims=True)
    weight_c = jnp.sqrt(overall / (float(strata_total) * jnp.maximum(stratum_c, 1.0)))
    eye = iota((examples, examples), 0) == iota((examples, examples), 1)
    weight = jnp.sum(jnp.where(eye, weight_c, 0.0), axis=0, keepdims=True)
    at_slot = (iota((rows, examples), 0) // kr).astype(F32) == slot
    square_e = jnp.sum(jnp.where(at_slot, square, 0.0), axis=0, keepdims=True)
    weight = weight * lax.rsqrt(square_e + EPSILON)

    scores_all = rbuf.at[pl.ds(0, n - 1)]
    pltpu.make_async_copy(scores_all, scores_all, rr).wait()
    home = ((c * nx + x) * nz + z) * CAP * kr
    raw = jnp.zeros((1, examples), F32)
    lane_row = iota((1, count), 1)
    for o in range(nz):
        top = jnp.max(rbuf[o * nt:(o + 1) * nt], axis=0)
        for rank in range(CAP):
            mine = jnp.sum(
                jnp.where(lane_row == home + rank * kr, top, 0.0), axis=1, keepdims=True)
            raw = jnp.where(slot == float(o * CAP + rank), mine, raw)
    out_ref[...] = jnp.where(sent, raw * weight, 0.0)

    def drain(ref, sem):
        pltpu.make_async_copy(ref, ref, sem).wait()

    drain(counts_all, ns)
    drain(scores_all, rs)
    for half in range(HALVES):
        if nz > 1:
            drain(sbuf.at[half, pl.ds(0, nz - 1)], zs.at[half])
        for _ in range(1, nx):
            drain(xbuf.at[half, 0, 0], xs.at[half])
        drain(xbuf.at[half, 0], cs.at[half])


def solution(mesh):
    nz, nt = mesh.shape["dp"], mesh.shape["tgt"]

    def shards(hidden, cotangent, adapter_down_weight, adapter_up_weight, width_projection_factor,
               rank_projection_factor, targets, strata, keep, shard_example_count,
               stratum_owner_table):
        tokens, width = hidden.shape
        rank, kr = rank_projection_factor.shape
        kd = width_projection_factor.shape[1]
        examples = strata.shape[0]
        strata_total = stratum_owner_table.shape[0]
        local_targets, feat = targets.shape[1:]
        n, nx = nz * nt, nt // CORES
        count = n * CAP * kr
        span = kr * 128
        count_lanes = -(-strata_total // 128) * 128
        dma = pltpu.SemaphoreType.DMA
        hbm = pl.BlockSpec(memory_space=pl.ANY)
        vmem = pl.BlockSpec(memory_space=pltpu.VMEM)
        smem = pl.BlockSpec(memory_space=pltpu.SMEM)

        def body(*refs):
            kernel(nz, nt, *refs)

        out = pl.pallas_call(
            body,
            name="select",
            out_shape=jax.ShapeDtypeStruct((1, examples), F32),
            in_specs=[hbm, hbm, hbm, hbm, hbm, vmem, hbm, vmem, vmem, smem, vmem],
            out_specs=vmem,
            scratch_shapes=[
                pltpu.VMEM((tokens, width), BF16),
                pltpu.VMEM((tokens, width), BF16),
                pltpu.VMEM((rank, width), BF16),
                pltpu.VMEM((rank, width), BF16),
                pltpu.VMEM((width, kd), BF16),
                pltpu.VMEM((kr, local_targets, kd), BF16),
                pltpu.VMEM((local_targets, feat // 2), BF16),
                pltpu.VMEM((kr, local_targets, kd), BF16),
                pltpu.VMEM((span, span), BF16),
                pltpu.VMEM((HALVES, nz, CAP * kr, 2 * kd // HALVES), BF16),
                pltpu.VMEM((HALVES, CORES, nx, nz, CAP * kr, 2 * kd // HALVES), BF16),
                pltpu.VMEM((local_targets, count), F32),
                pltpu.VMEM((1, count_lanes), F32),
                pltpu.VMEM((n, 1, count_lanes), F32),
                pltpu.VMEM((1, count), F32),
                pltpu.VMEM((n, 1, count), F32),
                dma((6, CHUNKS)),
                dma((kr + 1,)),
                dma((HALVES,)),
                dma((HALVES, nz)),
                dma((HALVES,)),
                dma((HALVES, nx, nz)),
                dma((HALVES,)),
                dma((HALVES,)),
                dma,
                dma,
                dma,
                dma,
            ],
            compiler_params=pltpu.CompilerParams(
                collective_id=0, has_side_effects=True, vmem_limit_bytes=60 * 1024 * 1024),
        )(hidden, cotangent, adapter_down_weight.T, adapter_up_weight, width_projection_factor,
          rank_projection_factor.T, targets, strata.reshape(1, -1), keep.reshape(1, -1),
          shard_example_count, stratum_owner_table.reshape(1, -1))
        return out.reshape(-1)

    split = P(("groups", "dp", "tgt"))
    rows = P(("groups", "dp", "tgt"), None)
    return jax.shard_map(
        shards,
        mesh=mesh,
        in_specs=(rows, rows, P(), P(), P(), P(), P(("groups", "dp"), "tgt", None),
                  split, split, split, P()),
        out_specs=split,
        check_vma=False,
    )
```

```python
import math

import jax
import jax.numpy as jnp
from jax import lax
from jax.experimental import pallas as pl
from jax.experimental.pallas import tpu as pltpu
from jax.sharding import PartitionSpec as P

CAP = 2
TASKS = 16
EPSILON = 1e-06
CORES = 2
CHUNKS = 4
HALVES = 2

F32 = jnp.float32
BF16 = jnp.bfloat16
I32 = jnp.int32
MESH = pl.DeviceIdType.MESH


def dot(a, b):
    return jnp.dot(a, b, preferred_element_type=F32)


def dot_nt(a, b):
    return lax.dot_general(a, b, (((1,), (1,)), ((), ())), preferred_element_type=F32)


def iota(shape, axis):
    return lax.broadcasted_iota(I32, shape, axis)


def column_of(row):
    size = row.shape[1]
    eye = iota((size, size), 0) == iota((size, size), 1)
    return jnp.sum(jnp.where(eye, jnp.broadcast_to(row, (size, size)), 0.0), axis=1, keepdims=True)


def each(start, stop, body):
    if stop - start <= 32:
        for k in range(start, stop):
            body(k)
    else:
        lax.fori_loop(start, stop, lambda k, c: (body(k), c)[1], 0)


def partner(z, k, nz):
    if nz & (nz - 1):
        return lax.rem(z + k, nz)
    bit = 1
    while bit < nz:
        if k & bit:
            z = z + bit - 2 * bit * lax.rem(z // bit, 2)
        bit *= 2
    return z


def kernel(nz, nt, hid_h, cot_h, ad_h, au_h, w_h, rp_ref, tg_h, strata_ref, keep_ref,
           cnt_ref, table_ref, out_ref, hid, cot, ad, au, wf, tup, tdr, tdn, sel, sbuf, xbuf,
           acc, crow, cbuf, rrow, rbuf, in_sem, tg_sem, zs, zr, xs, xr, cs, cr, ns, nr, rs, rr):
    n = nz * nt
    nx = nt // CORES
    z = lax.axis_index("dp")
    t = lax.axis_index("tgt")
    me = z * nt + t
    x, c = t // CORES, lax.rem(t, CORES)
    tokens, width = hid.shape
    kd = wf.shape[1]
    hw = kd // HALVES
    kr = rp_ref.shape[0]
    examples = strata_ref.shape[1]
    seq = tokens // examples
    strata_total = table_ref.shape[1]
    local_targets = tdr.shape[0]
    slots = nz * CAP
    rows = slots * kr
    kc = width // CHUNKS

    def peer(j):
        return {"dp": j // nt, "tgt": lax.rem(j, nt)}

    barrier = pltpu.get_barrier_semaphore()
    for k in range(nz - 1, 0, -1):
        pl.semaphore_signal(
            barrier, inc=1, device_id={"dp": partner(z, k, nz)}, device_id_type=MESH)
    for dx in range(1, nx):
        pl.semaphore_signal(
            barrier, inc=1, device_id={"tgt": lax.rem(x + dx, nx) * CORES + c},
            device_id_type=MESH)
    pl.semaphore_signal(
        barrier, inc=1, device_id={"tgt": x * CORES + 1 - c}, device_id_type=MESH)

    def loads(k):
        ks = pl.ds(k * kc, kc)
        return [
            pltpu.make_async_copy(hid_h.at[:, ks], hid.at[:, ks], in_sem.at[0, k]),
            pltpu.make_async_copy(w_h.at[ks, pl.ds(0, hw)], wf.at[ks, pl.ds(0, hw)], in_sem.at[1, k]),
            pltpu.make_async_copy(cot_h.at[:, ks], cot.at[:, ks], in_sem.at[2, k]),
            pltpu.make_async_copy(ad_h.at[:, ks], ad.at[:, ks], in_sem.at[3, k]),
            pltpu.make_async_copy(au_h.at[:, ks], au.at[:, ks], in_sem.at[4, k]),
        ]

    def late_loads(k):
        ks = pl.ds(k * kc, kc)
        rest = pl.ds(hw, kd - hw)
        return [pltpu.make_async_copy(w_h.at[ks, rest], wf.at[ks, rest], in_sem.at[5, k])]

    first = [loads(k) for k in range(CHUNKS)]
    second = [late_loads(k) for k in range(CHUNKS)]
    up_len = kr * kd
    target_loads = [
        pltpu.make_async_copy(tg_h.at[0, :, pl.ds(r * kd, kd)], tup.at[r], tg_sem.at[r])
        for r in range(kr)
    ] + [pltpu.make_async_copy(tg_h.at[0, :, pl.ds(up_len, up_len)], tdr, tg_sem.at[kr])]
    for group in first + second:
        for copy in group:
            copy.start()
    for copy in target_loads:
        copy.start()

    strata = strata_ref[...].astype(F32)
    live = jnp.logical_and(keep_ref[...] == 1, iota((1, examples), 1) < cnt_ref[0])
    live_f = live.astype(F32)
    strata_c = column_of(strata)
    live_c = column_of(live_f)
    table_c = column_of(table_ref[...].astype(F32))
    member = strata == iota((strata_total, examples), 0).astype(F32)
    owner = jnp.sum(jnp.where(member, table_c, 0.0), axis=0, keepdims=True)
    owner_c = column_of(owner)
    earlier = iota((examples, examples), 0) < iota((examples, examples), 1)
    ahead = jnp.where(jnp.logical_and(earlier, owner_c == owner), live_c, 0.0)
    slot_rank = jnp.sum(ahead, axis=0, keepdims=True)
    sent = jnp.logical_and(live, slot_rank < float(CAP))
    slot = jnp.where(sent, owner * float(CAP) + slot_rank, -1.0)
    lanes = crow.shape[1]
    member_t = strata_c == iota((examples, lanes), 1).astype(F32)
    crow[...] = jnp.sum(jnp.where(member_t, live_c, 0.0), axis=0, keepdims=True)
    own_counts = crow[...]

    spread = (iota((examples, tokens), 1) // seq == iota((examples, tokens), 0)).astype(BF16)
    slot_tok = dot(jnp.broadcast_to(slot, (8, examples)).astype(BF16), spread)[0:1, :]
    row_slot = (iota((rows, tokens), 0) // kr).astype(F32)
    picked = row_slot == slot_tok
    row_rank = (
        lax.rem(iota((rows, kr), 0), kr) == iota((rows, kr), 1)
    ).astype(BF16)

    def count_copy(k):
        return pltpu.make_async_remote_copy(
            crow, cbuf.at[me], ns, nr, device_id=peer(lax.rem(me + k, n)), device_id_type=MESH)

    cbuf[me] = own_counts

    span = sel.shape[0]
    dd = span // kr
    dst = iota((1, span), 1)
    source = lax.rem(dst, dd) * kr + dst // dd
    sel[...] = (iota((span, span), 0) == source).astype(F32).astype(BF16)

    wide_h = wide_b = down = up = None
    for k in range(CHUNKS):
        for copy in first[k]:
            copy.wait()
        ks = pl.ds(k * kc, kc)
        h, b, w = hid[:, ks], cot[:, ks], wf[ks, 0:hw]
        terms = (dot(h, w), dot(b, w), dot_nt(h, ad[:, ks]), dot_nt(b, au[:, ks]))
        if k == 0:
            wide_h, wide_b, down, up = terms
        else:
            wide_h, wide_b, down, up = [
                a + p for a, p in zip((wide_h, wide_b, down, up), terms)]
    rank_down = dot_nt(down.astype(BF16), rp_ref[...]).astype(BF16)
    rank_up = dot_nt(up.astype(BF16), rp_ref[...]).astype(BF16)
    mix_up = jnp.where(picked, dot_nt(row_rank, rank_down), 0.0).astype(BF16)
    mix_down = jnp.where(picked, dot_nt(row_rank, rank_up), 0.0).astype(BF16)

    def z_copy(half, k):
        to = partner(z, k, nz)
        return pltpu.make_async_remote_copy(
            sbuf.at[half, to], xbuf.at[half, c, x, z], zs.at[half], zr.at[half, z],
            device_id={"dp": to}, device_id_type=MESH)

    def x_copy(half, src_ref, origin_z, to_x):
        return pltpu.make_async_remote_copy(
            src_ref, xbuf.at[half, c, x, origin_z], xs.at[half], xr.at[half, x, origin_z],
            device_id={"tgt": to_x * CORES + c}, device_id_type=MESH)

    def c_copy(half, src_ref, origin_x, origin_z):
        return pltpu.make_async_remote_copy(
            src_ref, xbuf.at[half, c, origin_x, origin_z], cs.at[half], cr.at[half],
            device_id={"tgt": x * CORES + 1 - c}, device_id_type=MESH)

    def spread_out(half, src_ref, origin_z):
        for dx in range(1, nx):
            x_copy(half, src_ref, origin_z, lax.rem(x + dx, nx)).start()
        c_copy(half, src_ref, x, origin_z).start()

    def features(half, wb, wh):
        up_f = dot(mix_up, wb.astype(BF16)).astype(BF16)
        down_f = dot(mix_down, wh.astype(BF16)).astype(BF16)
        sbuf[half, :, :, 0:hw] = up_f.reshape(nz, CAP * kr, hw)
        sbuf[half, :, :, hw:2 * hw] = down_f.reshape(nz, CAP * kr, hw)
        if half == 0:
            pl.semaphore_wait(barrier, nz + nx - 1)
        for k in range(1, nz):
            z_copy(half, k).start()
        spread_out(half, sbuf.at[half, z], z)
        xbuf[half, c, x, z] = sbuf[half, z]
        wide_u, wide_d = up_f.astype(F32), down_f.astype(F32)
        return jnp.sum(wide_u * wide_u + wide_d * wide_d, axis=1, keepdims=True)

    square = features(0, wide_b, wide_h)
    for k in range(CHUNKS):
        for copy in second[k]:
            copy.wait()
        ks = pl.ds(k * kc, kc)
        w = wf[ks, hw:kd]
        terms = (dot(hid[:, ks], w), dot(cot[:, ks], w))
        if k == 0:
            wide_h, wide_b = terms
        else:
            wide_h, wide_b = wide_h + terms[0], wide_b + terms[1]
    square = square + features(1, wide_b, wide_h)

    for copy in target_loads:
        copy.wait()

    def target_scales():
        total = None
        for r in range(kr):
            v = tup[r].astype(F32)
            total = v * v if total is None else total + v * v
        for q in range(up_len // kd):
            v = tdr[:, q * kd:(q + 1) * kd].astype(F32)
            total = total + v * v
        return math.sqrt(2.0 * up_len) * lax.rsqrt(
            jnp.sum(total, axis=1, keepdims=True) + EPSILON)

    def arrange(q):
        piece = dot(tdr[:, q * span:(q + 1) * span], sel[...]).astype(BF16)
        for r in range(kr):
            tdn[r, :, q * dd:(q + 1) * dd] = piece[:, r * dd:(r + 1) * dd]

    def relay_z(half, k):
        origin = partner(z, k, nz)
        pltpu.make_async_remote_copy(
            sbuf.at[half, origin], xbuf.at[half, c, x, origin], zs.at[half], zr.at[half, origin],
            device_id={"dp": origin}, device_id_type=MESH).wait_recv()
        spread_out(half, xbuf.at[half, c, x, origin], origin)

    def relay_x(half, dx, k):
        origin_x = lax.rem(x + dx, nx)
        origin_z = partner(z, k, nz)
        block = xbuf.at[half, c, origin_x, origin_z]
        pltpu.make_async_remote_copy(
            block, block, xs.at[half], xr.at[half, origin_x, origin_z],
            device_id={"tgt": origin_x * CORES + c}, device_id_type=MESH).wait_recv()
        c_copy(half, block, origin_x, origin_z).start()

    target_scale = target_scales()
    pieces = up_len // span
    todo = [lambda q=q: arrange(q) for q in range(pieces)]
    steps = []
    for half in range(HALVES):
        steps += [lambda half=half, k=k: relay_z(half, k) for k in range(1, nz)]
    done = 0
    for i, step in enumerate(steps):
        while done < pieces and done * len(steps) <= i * pieces:
            todo[done]()
            done += 1
        step()
    while done < pieces:
        todo[done]()
        done += 1
    for half in range(HALVES):
        for dx in range(1, nx):
            for k in range(nz):
                relay_x(half, dx, k)

    count = nx * nz * CORES * CAP * kr
    lane = iota((local_targets, count), 1)
    lane_rank = lax.rem(lane, kr)
    for half in range(HALVES):
        other = xbuf.at[half, 1 - c]
        pltpu.make_async_copy(other, other, cr.at[half]).wait()
        if half == 0:
            each(1, n, lambda k: count_copy(k).start())
        block = xbuf[half].reshape(count, 2 * hw)
        cols = slice(half * hw, (half + 1) * hw)
        left = tup[:, :, cols].reshape(kr * local_targets, hw)
        right = tdn[:, :, cols].reshape(kr * local_targets, hw)
        products = dot_nt(left, block[:, 0:hw]) + dot_nt(right, block[:, hw:2 * hw])
        products = products.reshape(kr, local_targets, count)
        s = products[0]
        for r in range(1, kr):
            s = jnp.where(lane_rank == r, products[r], s)
        if half == 0:
            acc[...] = s
        else:
            s = acc[...] + s
    shift = 1
    while shift < kr:
        s = s + pltpu.roll(s, count - shift, 1)
        shift *= 2
    per_task = local_targets * nt // TASKS
    s = jnp.maximum(s * target_scale, 0.0)
    local_tasks = local_targets // per_task
    best = jnp.sum(s[0:per_task], axis=0, keepdims=True)
    for k in range(1, local_tasks):
        best = jnp.maximum(
            best, jnp.sum(s[k * per_task:(k + 1) * per_task], axis=0, keepdims=True))
    rrow[...] = best / float(per_task)

    def score_copy(k):
        return pltpu.make_async_remote_copy(
            rrow, rbuf.at[me], rs, rr, device_id=peer(lax.rem(me + k, n)), device_id_type=MESH)

    each(1, n, lambda k: score_copy(k).start())
    rbuf[me] = rrow[...]

    counts_all = cbuf.at[pl.ds(0, n - 1)]
    pltpu.make_async_copy(counts_all, counts_all, nr).wait()
    counts = jnp.sum(cbuf[...], axis=0)
    overall = jnp.sum(counts, axis=1, keepdims=True)
    stratum_c = jnp.sum(jnp.where(member_t, counts, 0.0), axis=1, keepdims=True)
    weight_c = jnp.sqrt(overall / (float(strata_total) * jnp.maximum(stratum_c, 1.0)))
    eye = iota((examples, examples), 0) == iota((examples, examples), 1)
    weight = jnp.sum(jnp.where(eye, weight_c, 0.0), axis=0, keepdims=True)
    at_slot = (iota((rows, examples), 0) // kr).astype(F32) == slot
    square_e = jnp.sum(jnp.where(at_slot, square, 0.0), axis=0, keepdims=True)
    weight = weight * lax.rsqrt(square_e + EPSILON)

    scores_all = rbuf.at[pl.ds(0, n - 1)]
    pltpu.make_async_copy(scores_all, scores_all, rr).wait()
    home = ((c * nx + x) * nz + z) * CAP * kr
    raw = jnp.zeros((1, examples), F32)
    lane_row = iota((1, count), 1)
    for o in range(nz):
        top = jnp.max(rbuf[o * nt:(o + 1) * nt], axis=0)
        for rank in range(CAP):
            mine = jnp.sum(
                jnp.where(lane_row == home + rank * kr, top, 0.0), axis=1, keepdims=True)
            raw = jnp.where(slot == float(o * CAP + rank), mine, raw)
    out_ref[...] = jnp.where(sent, raw * weight, 0.0)

    def drain(ref, sem):
        pltpu.make_async_copy(ref, ref, sem).wait()

    drain(counts_all, ns)
    drain(scores_all, rs)
    for half in range(HALVES):
        if nz > 1:
            drain(sbuf.at[half, pl.ds(0, nz - 1)], zs.at[half])
        for _ in range(1, nx):
            drain(xbuf.at[half, 0, 0], xs.at[half])
        drain(xbuf.at[half, 0], cs.at[half])


def solution(mesh):
    nz, nt = mesh.shape["dp"], mesh.shape["tgt"]

    def shards(hidden, cotangent, adapter_down_weight, adapter_up_weight, width_projection_factor,
               rank_projection_factor, targets, strata, keep, shard_example_count,
               stratum_owner_table):
        tokens, width = hidden.shape
        rank, kr = rank_projection_factor.shape
        kd = width_projection_factor.shape[1]
        examples = strata.shape[0]
        strata_total = stratum_owner_table.shape[0]
        local_targets, feat = targets.shape[1:]
        n, nx = nz * nt, nt // CORES
        count = n * CAP * kr
        span = kr * 128
        count_lanes = -(-strata_total // 128) * 128
        dma = pltpu.SemaphoreType.DMA
        hbm = pl.BlockSpec(memory_space=pl.ANY)
        vmem = pl.BlockSpec(memory_space=pltpu.VMEM)
        smem = pl.BlockSpec(memory_space=pltpu.SMEM)

        def body(*refs):
            kernel(nz, nt, *refs)

        out = pl.pallas_call(
            body,
            name="select",
            out_shape=jax.ShapeDtypeStruct((1, examples), F32),
            in_specs=[hbm, hbm, hbm, hbm, hbm, vmem, hbm, vmem, vmem, smem, vmem],
            out_specs=vmem,
            scratch_shapes=[
                pltpu.VMEM((tokens, width), BF16),
                pltpu.VMEM((tokens, width), BF16),
                pltpu.VMEM((rank, width), BF16),
                pltpu.VMEM((rank, width), BF16),
                pltpu.VMEM((width, kd), BF16),
                pltpu.VMEM((kr, local_targets, kd), BF16),
                pltpu.VMEM((local_targets, feat // 2), BF16),
                pltpu.VMEM((kr, local_targets, kd), BF16),
                pltpu.VMEM((span, span), BF16),
                pltpu.VMEM((HALVES, nz, CAP * kr, 2 * kd // HALVES), BF16),
                pltpu.VMEM((HALVES, CORES, nx, nz, CAP * kr, 2 * kd // HALVES), BF16),
                pltpu.VMEM((local_targets, count), F32),
                pltpu.VMEM((1, count_lanes), F32),
                pltpu.VMEM((n, 1, count_lanes), F32),
                pltpu.VMEM((1, count), F32),
                pltpu.VMEM((n, 1, count), F32),
                dma((6, CHUNKS)),
                dma((kr + 1,)),
                dma((HALVES,)),
                dma((HALVES, nz)),
                dma((HALVES,)),
                dma((HALVES, nx, nz)),
                dma((HALVES,)),
                dma((HALVES,)),
                dma,
                dma,
                dma,
                dma,
            ],
            compiler_params=pltpu.CompilerParams(
                collective_id=0, has_side_effects=True, vmem_limit_bytes=60 * 1024 * 1024),
        )(hidden, cotangent, adapter_down_weight.T, adapter_up_weight, width_projection_factor,
          rank_projection_factor.T, targets, strata.reshape(1, -1), keep.reshape(1, -1),
          shard_example_count, stratum_owner_table.reshape(1, -1))
        return out.reshape(-1)

    split = P(("groups", "dp", "tgt"))
    rows = P(("groups", "dp", "tgt"), None)
    return jax.shard_map(
        shards,
        mesh=mesh,
        in_specs=(rows, rows, P(), P(), P(), P(), P(("groups", "dp"), "tgt", None),
                  split, split, split, P()),
        out_specs=split,
        check_vma=False,
    )
```
